256 devices in a mesh: seq: 32 (over z_hi, y, core), fsdp: 8 (over z_lo, x).
Axes of the slice: x: 4, y: 4, z: 8 (z_hi: 4, z_lo: 2; z = z_hi * 2 + z_lo), core: 2. Of those that a mesh axis runs over, the one named last changes fastest.
Arguments:
- tokens: bfloat16 [32768, 1280], P('seq'), may hold values from -64 to 64
- cotangent: bfloat16 [32768, 1280], P('seq'), may hold values from -6 to 6
- raster_dest: int32 [32768], P('seq'), may hold values from 0 to 32767, as said below
- keep_mask: int32 [512, 16, 4096], P('seq', 'fsdp'), may hold values 0 or 1
- qkv_weight: bfloat16 [1280, 3840], P('seq', 'fsdp'), may hold values from -0.15625 to 0.15625
- out_weight: bfloat16 [1280, 1280], P('seq', 'fsdp'), may hold values from -0.15625 to 0.15625
Outputs:
- attended: bfloat16 [32768, 1280], P('seq', 'fsdp')
- grad_tokens: bfloat16 [32768, 1280], P('seq', 'fsdp')
- grad_qkv: float32 [1280, 3840], P('seq', 'fsdp')
- grad_out: float32 [1280, 1280], P('seq', 'fsdp')
The draws below stay inside these ranges and needn't reach their ends.
Inputs may be any that keep to these rules, and one draw needn't show every extreme that they name: `raster_dest`: A permutation. Raster rows form bands of 2048 rows (8 patch rows of 256 patches); band b holds 32 windows of 8 by 8 patches, which go one to each block of 1024 window-order rows, in an order drawn for each band; inside its block, band b's window takes rows b * 64 to (b + 1) * 64 - 1, its patches in raster order.
All inputs are finite; a program needn't handle non-finite values. No bound on the sum of `keep_mask` on one device may be relied on, other than what follows from the above.
Results may differ from the reference program's by a relative error of at most 0.025.
The reference program's roundings to bfloat16 on the way count: a program that leaves them out, or rounds other values in their place, can miss the bound.
Values may be sent and summed in bfloat16 or wider, within the bound.
No kernel may reach another device: no remote copies, remote signals or barrier semaphores. Data moves between devices by JAX's collectives and lax.ppermute only.
A program may use at most 64 MiB of HBM per device.

```python
import jax
import jax.numpy as jnp
from jax import lax

D = 1280
HEADS = 16
HEAD_DIM = 80
WIN = 8
TOK_DEV = 1024
WIN_TOK = 64
IMG_W = 256
TOKENS = 32768
WINDOWS = 512
N_SEQ = 32
N_FSDP = 8


def draw_tokens(key, part):
    first_key = jax.random.fold_in(key, 0)
    normal_part = jax.random.truncated_normal(first_key, -6.0, 6.0, (TOKENS, D), jnp.float32)
    return normal_part.astype(jnp.bfloat16)


def band_order(band_key):
    return jax.random.permutation(band_key, N_SEQ)


def draw_raster_dest(key, part):
    band_count = TOKENS // (WIN_TOK * N_SEQ)
    band_keys = jax.random.split(key, band_count)
    orders = jax.vmap(band_order)(band_keys)
    row_index = jnp.arange(TOKENS, dtype=jnp.int32)
    band_len = WIN_TOK * N_SEQ
    band_index = row_index // band_len
    inside_band = row_index % band_len
    patch_row = inside_band // IMG_W
    patch_col = inside_band % IMG_W
    target = orders[band_index, patch_col // WIN]
    local_slot = band_index * WIN_TOK + patch_row * WIN + patch_col % WIN
    return (target * TOK_DEV + local_slot).astype(jnp.int32)


def place_ends(drawn, key, smallest, top_value):
    extent = drawn.shape
    place = [jax.random.randint(jax.random.fold_in(key, axis), (), 0, extent[axis]) for axis in range(len(extent))]
    drawn = drawn.at[tuple(place)].set(smallest)
    longest = extent.index(max(extent))
    place[longest] = (place[longest] + 1) % extent[longest]
    return drawn.at[tuple(place)].set(top_value)


def levels(stream_key, dims, pieces, low, top_value):
    level, own = 1.0, jax.random.fold_in(stream_key, 6)
    for dim, parts in pieces:
        heights = jnp.exp(jax.random.uniform(jax.random.fold_in(own, dim), (parts,), jnp.float32, low / len(pieces), top_value / len(pieces)))
        level = level * jnp.repeat(heights, dims[dim] // parts).reshape([-1 if axis == dim else 1 for axis in range(len(dims))])
    return level


def noise(own_key, extent, width, most, cuts=(), held_as=jnp.bfloat16):
    loudness = levels(own_key, extent, cuts, -0.22, 0.18) if cuts else 1.0
    entries = jax.random.normal(own_key, extent, jnp.float32) * width * loudness
    return jnp.minimum(jnp.maximum(entries, -most), most).astype(held_as)


def setup_inputs(seed: int = 0) -> dict:
    keys = jax.random.split(jax.random.key(seed), 7)
    tokens = draw_tokens(jax.random.fold_in(keys[6], 71), 0)
    cotangent = noise(keys[1], (TOKENS, D), 1.0, 6.0, ((0, 32),))
    raster_dest = draw_raster_dest(jax.random.fold_in(keys[6], 71), 0)
    keep_mask = place_ends((jax.random.randint(keys[3], (WINDOWS, HEADS, WIN_TOK * WIN_TOK), 0, 10) < 9).astype(jnp.int32), jax.random.fold_in(keys[3], 1), 0, 1)
    qkv_weight = noise(keys[4], (D, 3 * D), D ** -0.5, 0.15625, ((0, 32), (1, 8)))
    out_weight = noise(keys[5], (D, D), D ** -0.5, 0.15625, ((0, 32), (1, 8)))
    return {"tokens": tokens, "cotangent": cotangent, "raster_dest": raster_dest, "keep_mask": keep_mask, "qkv_weight": qkv_weight, "out_weight": out_weight}


INV_KEEP = 1.0 / 0.9


def to_half(values):
    return lax.optimization_barrier(values.astype(jnp.bfloat16))


def reference(tokens, cotangent, raster_dest, keep_mask, qkv_weight, out_weight):
    score_scale = HEAD_DIM ** -0.5
    windowed = jnp.zeros_like(tokens).at[raster_dest].set(tokens)
    cot_window = jnp.zeros_like(cotangent).at[raster_dest].set(cotangent)
    projected = to_half(jnp.dot(windowed, qkv_weight, preferred_element_type=jnp.float32))
    unpacked = projected.reshape(WINDOWS, WIN_TOK, HEADS, 3, HEAD_DIM).astype(jnp.float32)
    queries = unpacked[:, :, :, 0].transpose(0, 2, 1, 3)
    key_rows = unpacked[:, :, :, 1].transpose(0, 2, 1, 3)
    value_rows = unpacked[:, :, :, 2].transpose(0, 2, 1, 3)
    keep_scale = keep_mask.reshape(WINDOWS, HEADS, WIN_TOK, WIN_TOK).astype(jnp.float32) * INV_KEEP
    scores = jnp.einsum("whqe,whke->whqk", queries, key_rows) * score_scale
    attn_probs = jax.nn.softmax(scores, axis=-1)
    dropped = to_half(attn_probs * keep_scale).astype(jnp.float32)
    mixed = to_half(jnp.einsum("whqk,whke->whqe", dropped, value_rows))
    mixed_heads = mixed.transpose(0, 2, 1, 3).reshape(TOKENS, D)
    grad_heads = to_half(jnp.dot(cot_window, out_weight, preferred_element_type=jnp.float32))
    grad_rows = grad_heads.reshape(WINDOWS, WIN_TOK, HEADS, HEAD_DIM).transpose(0, 2, 1, 3).astype(jnp.float32)
    grad_probs = jnp.einsum("whqe,whke->whqk", grad_rows, value_rows) * keep_scale
    inner = jnp.sum(grad_probs * attn_probs, axis=-1, keepdims=True)
    grad_scores = to_half(score_scale * attn_probs * (grad_probs - inner)).astype(jnp.float32)
    grad_query = jnp.einsum("whqk,whke->whqe", grad_scores, key_rows)
    grad_key = jnp.einsum("whqk,whqe->whke", grad_scores, queries)
    grad_value = jnp.einsum("whqk,whqe->whke", dropped, grad_rows)
    stacked = jnp.stack([grad_query, grad_key, grad_value], axis=3)
    grad_projected = stacked.transpose(0, 2, 1, 3, 4).reshape(TOKENS, 3 * D).astype(jnp.bfloat16)
    col_width = D // N_FSDP
    out_total = jnp.zeros((TOKENS, D), jnp.float32)
    back_total = jnp.zeros((TOKENS, D), jnp.float32)
    contract = (((1,), (1,)), ((), ()))
    for group_index in range(N_FSDP):
        low = group_index * col_width
        qlow = group_index * 3 * col_width
        out_partial = lax.dot_general(mixed_heads[:, low:low + col_width], out_weight[:, low:low + col_width], contract, preferred_element_type=jnp.float32)
        out_total = out_total + to_half(out_partial).astype(jnp.float32)
        back_partial = lax.dot_general(grad_projected[:, qlow:qlow + 3 * col_width], qkv_weight[:, qlow:qlow + 3 * col_width], contract, preferred_element_type=jnp.float32)
        back_total = back_total + to_half(back_partial).astype(jnp.float32)
    attended = out_total.astype(jnp.bfloat16)[raster_dest]
    grad_tokens = back_total.astype(jnp.bfloat16)[raster_dest]
    grad_scale = TOKENS ** -0.5
    over_rows = (((0,), (0,)), ((), ()))
    grad_qkv = lax.dot_general(windowed, grad_projected, over_rows, preferred_element_type=jnp.float32) * grad_scale
    grad_out = lax.dot_general(cot_window, mixed_heads, over_rows, preferred_element_type=jnp.float32) * grad_scale
    return (attended, grad_tokens, grad_qkv, grad_out)
```

```python
import functools

import jax
import jax.numpy as jnp
from jax import lax
from jax.experimental import pallas as pl
from jax.experimental.pallas import tpu as pltpu
from jax.sharding import Mesh
from jax.sharding import PartitionSpec as P

D = 1280
HEAD_DIM = 80
WIN_TOK = 64
TOK_DEV = 1024
PAIR = 128
INV_KEEP = 1.0 / 0.9
SCORE_SCALE = HEAD_DIM**-0.5
BF = jnp.bfloat16
F32 = jnp.float32
NT = (((1,), (1,)), ((), ()))
TN = (((0,), (0,)), ((), ()))
ANY = pl.BlockSpec(memory_space=pl.ANY)
VMEM = pl.BlockSpec(memory_space=pltpu.VMEM)
SMEM = pl.BlockSpec(memory_space=pltpu.SMEM)


def params(mib):
    return pltpu.CompilerParams(vmem_limit_bytes=mib << 20)


def cost(flops, moved):
    return pl.CostEstimate(flops=flops, bytes_accessed=moved, transcendentals=0)


def dot(a, b, dims=None):
    if dims is None:
        dims = (((1,), (0,)), ((), ()))
    return lax.dot_general(a, b, dims, preferred_element_type=F32)


def pick_kernel(idx_ref, tok_ref, cot_ref, out_ref, sems):
    row = idx_ref[16]
    copies = []
    for k in range(16):
        window = idx_ref[k]
        for a, src in enumerate((tok_ref, cot_ref)):
            copies.append(
                pltpu.make_async_copy(
                    src.at[row, window], out_ref.at[k, a], sems.at[2 * k + a]
                )
            )
    for copy in copies:
        copy.start()
    for copy in copies:
        copy.wait()


def pick(idx, tokens, cotangent):
    view = (4, 32, 8, D)
    return pl.pallas_call(
        pick_kernel,
        out_shape=jax.ShapeDtypeStruct((16, 2, 8, D), BF),
        in_specs=[SMEM, ANY, ANY],
        out_specs=ANY,
        scratch_shapes=[pltpu.SemaphoreType.DMA((32,))],
        cost_estimate=cost(0, 1 << 21),
        name="pick_rows",
    )(idx, tokens.reshape(view), cotangent.reshape(view))


def weights_kernel(idx_ref, w0, w1, w2, w3, wp_ref, op_ref, a_ref, b_ref, full, sems):
    z, y = idx_ref[0], idx_ref[1]
    copies = []
    for k, src in enumerate((w0, w1, w2, w3)):
        y_from = lax.rem(y - k + 4, 4)
        for m in range(8):
            z_from = lax.rem(z - m + 8, 8)
            slot = (z_from // 2) * 8 + y_from * 2 + lax.rem(z_from, 2)
            copies.append(
                pltpu.make_async_copy(src.at[m], full.at[slot], sems.at[8 * k + m])
            )
    for copy in copies:
        copy.start()
    for copy in copies:
        copy.wait()
    i = lax.broadcasted_iota(jnp.int32, (640, 768), 0)
    j = lax.broadcasted_iota(jnp.int32, (640, 768), 1)
    spread = jnp.where((j % 128 < HEAD_DIM) & (i == j // 128 * HEAD_DIM + j % 128), 1.0, 0.0)
    spread = spread.astype(BF)
    i = lax.broadcasted_iota(jnp.int32, (640, 256), 0)
    j = lax.broadcasted_iota(jnp.int32, (640, 256), 1)
    spread_out = jnp.where(
        (j % 128 < HEAD_DIM) & (i == 480 + j // 128 * HEAD_DIM + j % 128), 1.0, 0.0
    ).astype(BF)
    for r in range(4):
        rows = full[8 * r : 8 * r + 8].reshape(320, 640)
        wp_ref[pl.ds(320 * r, 320), :] = dot(rows, spread).astype(BF)
        op_ref[pl.ds(320 * r, 320), :] = dot(rows, spread_out).astype(BF)
    for g in range(4):
        lo, hi = g * 160, (4 + g) * 160
        a_ref[g, 0:160, :] = op_ref[lo : lo + 160, :]
        a_ref[g, 160:256, :] = jnp.zeros((96, 256), BF)
        a_ref[g, 256:416, :] = op_ref[hi : hi + 160, :]
        a_ref[g, 416:512, :] = jnp.zeros((96, 256), BF)
        b_ref[g, 0:32, :] = jnp.zeros((32, 768), BF)
        b_ref[g, 32:192, :] = wp_ref[lo : lo + 160, :]
        b_ref[g, 192:256, :] = wp_ref[hi + 96 : hi + 160, :]
        b_ref[g, 256:288, :] = jnp.zeros((32, 768), BF)
        b_ref[g, 288:384, :] = wp_ref[hi : hi + 96, :]


def arrange_weights(idx, pieces):
    shape = jax.ShapeDtypeStruct
    return pl.pallas_call(
        weights_kernel,
        out_shape=(
            shape((D, 768), BF),
            shape((D, 256), BF),
            shape((4, 512, 256), BF),
            shape((4, 384, 768), BF),
        ),
        in_specs=[SMEM] + [ANY] * 4,
        out_specs=(VMEM,) * 4,
        scratch_shapes=[pltpu.VMEM((32, 40, 640), BF), pltpu.SemaphoreType.DMA((32,))],
        compiler_params=params(40),
        cost_estimate=cost(2 * D * 640 * 1024, 8 << 20),
        name="arrange_weights",
    )(idx, *pieces)


def layer_kernel(
    idx_ref, *refs
):
    pieces = refs[:8]
    wp_ref, op_ref, a_ref, b_ref, keep_ref = refs[8:13]
    mine = refs[13:17]
    other = refs[17:21]
    grads = refs[21:25]
    x_ref, c_ref, gp_ref, mix_ref, z_ref, g_ref, g1_ref, m1_ref, in_sems, out_sems = refs[25:]
    core, x_pos, y_pos = idx_ref[0], idx_ref[1], idx_ref[2]
    copies = []
    for half in range(2):
        for k in range(4):
            src = pieces[4 * half + k]
            which = core if half == 0 else 1 - core
            row = pl.multiple_of((4 * which + lax.rem(x_pos - k + 4, 4)) * 8, 8)
            for a, dst in enumerate((x_ref, c_ref)):
                copies.append(
                    pltpu.make_async_copy(
                        src.at[:, a], dst.at[:, pl.ds(row, 8), :], in_sems.at[2 * (4 * half + k) + a]
                    )
                )
    for copy in copies:
        copy.start()
    for copy in copies:
        copy.wait()

    row_half = lax.broadcasted_iota(jnp.int32, (PAIR, PAIR), 0) // WIN_TOK
    col_half = lax.broadcasted_iota(jnp.int32, (PAIR, PAIR), 1) // WIN_TOK
    same = row_half == col_half

    def block(i, carry):
        rows = pl.ds(pl.multiple_of(i * 256, 256), 256)
        xs = x_ref[pl.ds(4 * i, 4)].reshape(256, D)
        cs = c_ref[pl.ds(4 * i, 4)].reshape(256, D)
        projected = dot(xs, wp_ref[...]).astype(BF)
        grad_heads = dot(cs, op_ref[...]).astype(BF)
        for pair in range(2):
            lo = pair * PAIR
            for h in range(2):
                q = projected[lo : lo + PAIR, h * 384 : h * 384 + 128]
                k = projected[lo : lo + PAIR, h * 384 + 128 : h * 384 + 256]
                v = projected[lo : lo + PAIR, h * 384 + 256 : h * 384 + 384]
                g = grad_heads[lo : lo + PAIR, h * 128 : h * 128 + 128]
                scores = jnp.where(same, dot(q, k, NT) * SCORE_SCALE, -1e30)
                top = jnp.max(scores, axis=-1, keepdims=True)
                e = jnp.exp(scores - top)
                probs = e / jnp.sum(e, axis=-1, keepdims=True)
                keep = keep_ref[2 * i + pair, h].astype(F32) * INV_KEEP
                dropped = (probs * keep).astype(BF)
                mixed = dot(dropped, v).astype(BF)
                gprobs = dot(g, v, NT) * keep
                inner = jnp.sum(gprobs * probs, axis=-1, keepdims=True)
                ds = (SCORE_SCALE * probs * (gprobs - inner)).astype(BF)
                at = pl.ds(pl.multiple_of(i * 256 + lo, PAIR), PAIR)
                mix_ref[at, h * 128 : h * 128 + 128] = mixed
                gp_ref[at, h * 384 : h * 384 + 128] = dot(ds, k).astype(BF)
                gp_ref[at, h * 384 + 128 : h * 384 + 256] = dot(ds, q, TN).astype(BF)
                gp_ref[at, h * 384 + 256 : h * 384 + 384] = dot(dropped, g, TN).astype(BF)
        mixed = mix_ref[rows, :]
        grad_projected = gp_ref[rows, :]
        for k in range(4):
            group = lax.rem(x_pos + k, 4)
            out = dot(mixed, a_ref[group], NT)
            back = dot(grad_projected, b_ref[group], NT)
            at = pl.ds(4 * i, 4)
            z_ref[k, at, :, 0:128] = out[:, 0:128].astype(BF).reshape(4, 64, 128)
            z_ref[k, at, :, 128:256] = (out[:, 128:256] + back[:, 0:128]).astype(BF).reshape(4, 64, 128)
            z_ref[k, at, :, 256:384] = back[:, 128:256].astype(BF).reshape(4, 64, 128)
            z_ref[k, at, :, 384:512] = out[:, 256:384].astype(BF).reshape(4, 64, 128)
            z_ref[k, at, :, 512:640] = (out[:, 384:512] + back[:, 256:384]).astype(BF).reshape(4, 64, 128)
        return carry

    lax.fori_loop(0, 4, block, 0)

    sends = []
    for k in range(4):
        own = pl.ds(pl.multiple_of(32 * core, 32), 32)
        rest = pl.ds(pl.multiple_of(32 * (1 - core), 32), 32)
        sends.append(pltpu.make_async_copy(z_ref.at[k, :, rest, :], other[k], out_sems.at[2 * k]))
        sends.append(pltpu.make_async_copy(z_ref.at[k, :, own, :], mine[k], out_sems.at[2 * k + 1]))
    for copy in sends:
        copy.start()

    i = lax.broadcasted_iota(jnp.int32, (768, 512), 0)
    j = lax.broadcasted_iota(jnp.int32, (768, 512), 1)
    tight = jnp.where((i % 128 < HEAD_DIM) & (j == i // 128 * HEAD_DIM + i % 128), 1.0, 0.0)
    tight = tight.astype(BF)
    i = lax.broadcasted_iota(jnp.int32, (256, 256), 0)
    j = lax.broadcasted_iota(jnp.int32, (256, 256), 1)
    tight_out = jnp.where(
        (i % 128 < HEAD_DIM) & (j == 96 + i // 128 * HEAD_DIM + i % 128), 1.0, 0.0
    ).astype(BF)
    g1_ref[...] = dot(gp_ref[...], tight).astype(BF)
    m1_ref[...] = dot(mix_ref[...], tight_out).astype(BF)

    for d in range(5):
        cols = slice(256 * d, 256 * d + 256)
        ga = dot(x_ref[:, :, cols].reshape(TOK_DEV, 256), g1_ref[...], TN)
        gb = dot(c_ref[:, :, cols].reshape(TOK_DEV, 256), m1_ref[...], TN)
        g_ref[cols, 0:384] = ga[:, 0:384].astype(BF)
        g_ref[cols, 384:512] = (ga[:, 384:512] + gb[:, 0:128]).astype(BF)
        g_ref[cols, 512:640] = gb[:, 128:256].astype(BF)
    for k in range(4):
        for zh in range(4):
            start = pl.multiple_of(320 * zh + 80 * lax.rem(y_pos + k, 4), 16)
            sends.append(
                pltpu.make_async_copy(
                    g_ref.at[pl.ds(start, 80), :], grads[k].at[zh], out_sems.at[8 + 4 * k + zh]
                )
            )
            sends[-1].start()
    for copy in sends:
        copy.wait()


def layer(idx, pieces, weights, keep):
    half = jax.ShapeDtypeStruct((16, 32, 640), BF)
    quarter = jax.ShapeDtypeStruct((4, 80, 640), BF)
    outs = pl.pallas_call(
        layer_kernel,
        out_shape=(half,) * 8 + (quarter,) * 4,
        in_specs=[SMEM] + [ANY] * 8 + [VMEM] * 5,
        out_specs=(ANY,) * 12,
        scratch_shapes=[
            pltpu.VMEM((16, WIN_TOK, D), BF),
            pltpu.VMEM((16, WIN_TOK, D), BF),
            pltpu.VMEM((TOK_DEV, 768), BF),
            pltpu.VMEM((TOK_DEV, 256), BF),
            pltpu.VMEM((4, 16, WIN_TOK, 640), BF),
            pltpu.VMEM((D, 640), BF),
            pltpu.VMEM((TOK_DEV, 512), BF),
            pltpu.VMEM((TOK_DEV, 256), BF),
            pltpu.SemaphoreType.DMA((16,)),
            pltpu.SemaphoreType.DMA((24,)),
        ],
        compiler_params=params(56),
        cost_estimate=cost(12 << 30, 24 << 20),
        name="layer",
    )(idx, *pieces, *weights, keep)
    return outs[0:4], outs[4:8], outs[8:12]


def total_kernel(p0, p1, p2, p3, p4, out_ref):
    def step(w, carry):
        total = p0[w].astype(F32) + p1[w].astype(F32)
        for p in (p2, p3, p4):
            total = total + p[w].astype(F32)
        total = total.astype(BF)
        out_ref[w, 0] = total[:, 0:384]
        out_ref[w, 1, :, 0:256] = total[:, 384:640]
        out_ref[w, 1, :, 256:384] = total[:, 256:384]
        return carry

    lax.fori_loop(0, 16, step, 0)


def total(parts):
    return pl.pallas_call(
        total_kernel,
        out_shape=jax.ShapeDtypeStruct((16, 2, 32, 384), BF),
        in_specs=[VMEM] * 5,
        out_specs=VMEM,
        compiler_params=params(16),
        cost_estimate=cost(1 << 21, 4 << 20),
        name="total",
    )(*parts)


def restore_kernel(idx_ref, got_ref, att_ref, back_ref):
    z_lo = idx_ref[32]

    def step(j, carry):
        rows = got_ref[idx_ref[j]]
        last = rows[:, 256:384].astype(F32)
        last = jnp.where(z_lo == 0, last, pltpu.roll(last, 64, 1)).astype(BF)
        att = rows[:, 0:160]
        back = jnp.concatenate([rows[:, 160:256], last[:, 0:64]], axis=1)
        for r in range(4):
            at = pl.ds(pl.multiple_of(j * 8, 8), 8)
            att_ref[r, at, :] = att[8 * r : 8 * r + 8]
            back_ref[r, at, :] = back[8 * r : 8 * r + 8]
        return carry

    lax.fori_loop(0, 32, step, 0)


def restore(idx, got):
    shape = jax.ShapeDtypeStruct((4, 256, 160), BF)
    att, back = pl.pallas_call(
        restore_kernel,
        out_shape=(shape, shape),
        in_specs=[SMEM, VMEM],
        out_specs=(VMEM, VMEM),
        compiler_params=params(16),
        cost_estimate=cost(0, 2 << 20),
        name="restore",
    )(idx, got)
    return att.reshape(TOK_DEV, 160), back.reshape(TOK_DEV, 160)


def shift(value, axis, size, k):
    return lax.ppermute(value, axis, [(i, (i + k) % size) for i in range(size)])


def swap(value):
    return lax.ppermute(value, ("c", "zl"), [(0, 0), (1, 2), (2, 1), (3, 3)])


def per_device(tokens, cotangent, raster_dest, keep_mask, qkv_weight, out_weight):
    core, x_pos, y_pos = lax.axis_index("c"), lax.axis_index("x"), lax.axis_index("y")
    z_hi, z_lo = lax.axis_index("zh"), lax.axis_index("zl")
    owner = raster_dest[:256].reshape(32, 8)[:, 0] // TOK_DEV
    window = jnp.arange(32, dtype=jnp.int32)
    wanted = 2 * jnp.arange(16, dtype=jnp.int32) + z_lo
    chosen = jnp.max(jnp.where(owner[None, :] == wanted[:, None], window[None, :], 0), axis=1)
    sent = pick(jnp.concatenate([chosen, x_pos[None]]), tokens, cotangent)
    got = lax.all_to_all(sent, ("zh", "y"), split_axis=0, concat_axis=0, tiled=True)

    shard = swap(jnp.concatenate([qkv_weight, out_weight], axis=1))
    column = [shard] + [shift(shard, ("zh", "zl"), 8, k) for k in range(1, 8)]
    column = jnp.stack(column)
    quarters = [column] + [shift(column, "y", 4, k) for k in range(1, 4)]
    weights = arrange_weights(jnp.stack([2 * z_hi + z_lo, y_pos]), quarters)

    keep = swap(keep_mask.astype(BF)).reshape(8, 2, 2, WIN_TOK, WIN_TOK).transpose(0, 2, 1, 3, 4)
    zeros = jnp.zeros((8, 2, WIN_TOK, WIN_TOK), BF)
    keep = jnp.concatenate(
        [
            jnp.concatenate([keep[:, :, 0], zeros], axis=-1),
            jnp.concatenate([zeros, keep[:, :, 1]], axis=-1),
        ],
        axis=-2,
    )

    row = [got] + [shift(got, "x", 4, k) for k in range(1, 4)]
    pieces = row + [shift(piece, "c", 2, 1) for piece in row]
    mine, other, grads = layer(jnp.stack([core, x_pos, y_pos]), pieces, weights, keep)

    parts = [mine[0], shift(other[0], "c", 2, 1)]
    for k in (2, 1, 3):
        both = mine[k].astype(F32) + shift(other[k], "c", 2, 1).astype(F32)
        parts.append(shift(both.astype(BF), "x", 4, k))
    message = total(parts).reshape(32, 32, 384)
    back = lax.all_to_all(message, ("zh", "y", "zl"), split_axis=0, concat_axis=0, tiled=True)
    attended, grad_tokens = restore(jnp.concatenate([owner, z_lo[None]]), back)

    summed = grads[0].astype(F32)
    for k in range(1, 4):
        summed = summed + shift(grads[k], "y", 4, k).astype(F32)
    spread = lax.all_to_all(
        summed.astype(BF).reshape(8, 40, 640), ("zh", "zl"), split_axis=0, concat_axis=0, tiled=True
    )
    grad = swap(jnp.sum(spread.astype(F32), axis=0) * (TOK_DEV * 32) ** -0.5)
    return attended, grad_tokens, grad[:, :480], grad[:, 480:]


def solution(mesh):
    fine = Mesh(mesh.devices.reshape(4, 4, 2, 2, 4), ("zh", "y", "c", "zl", "x"))
    seq, fsdp = ("zh", "y", "c"), ("zl", "x")
    return jax.shard_map(
        per_device,
        mesh=fine,
        in_specs=(
            P(seq, None),
            P(seq, None),
            P(seq),
            P(seq, fsdp, None),
            P(seq, fsdp),
            P(seq, fsdp),
        ),
        out_specs=(P(seq, fsdp),) * 4,
        check_vma=False,
    )
```
